128 devices in a mesh: gx: 8 (over y_lo, z), gy: 16 (over x, y_hi, core).
Axes of the slice: x: 4, y: 4 (y_hi: 2, y_lo: 2; y = y_hi * 2 + y_lo), z: 4, core: 2. Of those that a mesh axis runs over, the one named last changes fastest.
Arguments:
- adjoint: bfloat16 [600, 512, 1024], P(None, 'gy', 'gx'), may hold values from -48 to 48
- seafloor_depth: float32 [512, 1024], P('gy', 'gx'), may hold values from 0.5 to 2
- sensor_row: int32 [600], replicated, may hold values from 0 to 1023
- sensor_column: int32 [600], replicated, may hold values from 0 to 511
- noise_sigma: float32 [600], replicated, may hold values from 0.15 to 0.6
Outputs:
- gain_field: bfloat16 [600, 512, 1024], P(None, 'gy', 'gx')
The draws below stay inside these ranges and needn't reach their ends.
All inputs are finite; a program needn't handle non-finite values. Where the reference program divides by a largest or mean magnitude, that divisor is 1e-20 or more.
Results may differ from the reference program's by a relative error of at most 0.0052.
The reference program's roundings to bfloat16 on the way count: a program that leaves them out, or rounds other values in their place, can miss the bound.
Values may be sent and summed in bfloat16 or wider, within the bound.
A program may use at most 128 MiB of HBM per device.

```python
import math
import jax
import jax.numpy as jnp
from jax import lax

S = 600
SWEEPS = 4
ITERS = 4
NR = 1024
NC = 512
N_GX = 8


def sensor_sites(key):
    row_sites = jax.random.randint(jax.random.fold_in(key, 101), (S,), 0, NR)
    column_sites = jax.random.randint(jax.random.fold_in(key, 202), (S,), 0, NC)
    return (row_sites, column_sites)


def draw_sensor_row(key, part):
    return sensor_sites(key)[0]


def draw_sensor_column(key, part):
    return sensor_sites(key)[1]


def draw_adjoint(key, part):
    row_sites, column_sites = sensor_sites(key)
    noise_key = jax.random.fold_in(key, 303)
    first_partner = jax.random.permutation(jax.random.fold_in(key, 404), S)
    second_partner = jax.random.permutation(jax.random.fold_in(key, 505), S)
    row_axis = jnp.arange(NR).astype(jnp.float32)
    column_axis = jnp.arange(NC).astype(jnp.float32)

    def white(which):
        return jnp.clip(jax.random.normal(jax.random.fold_in(noise_key, which), (NC, NR), jnp.float32), -4.0, 4.0)

    def one_sensor(sensor):
        mixed = white(sensor) + 0.7 * white(first_partner[sensor]) + 0.5 * white(second_partner[sensor])
        column_reach = jnp.exp(-4.0 * jnp.abs(column_axis - column_sites[sensor].astype(jnp.float32)) / NC)
        row_reach = jnp.exp(-4.0 * jnp.abs(row_axis - row_sites[sensor].astype(jnp.float32)) / NR)
        envelope = 0.3 + 1.5 * column_reach[:, None] * row_reach[None, :]
        return envelope * mixed
    fields = lax.map(one_sensor, jnp.arange(S))
    return fields.astype(jnp.bfloat16)


def block_levels(rng, shape, shards, low, largest):
    level = 1.0
    for axis_at, parts in shards:
        heights = jax.random.uniform(jax.random.fold_in(jax.random.fold_in(rng, 6), axis_at), (parts,), jnp.float32, low / len(shards), largest / len(shards))
        level = level * jnp.repeat(jnp.exp(heights), shape[axis_at] // parts).reshape((-1,) + (1,) * (len(shape) - 1 - axis_at))
    return level


def setup_inputs(seed: int = 0) -> dict:
    keys = jax.random.split(jax.random.key(seed), 6)
    return {
        "adjoint": draw_adjoint(jax.random.fold_in(keys[5], 71), 0),
        "seafloor_depth": jnp.clip(jnp.exp(math.log(2.0) - 1.3862944 * jax.random.uniform(keys[1], (NC, NR), jnp.float32) ** block_levels(keys[1], (NC, NR), ((0, 16), (1, 8)), -0.2, 0.2)), 0.5, 2.0),
        "sensor_row": draw_sensor_row(jax.random.fold_in(keys[5], 71), 0),
        "sensor_column": draw_sensor_column(jax.random.fold_in(keys[5], 71), 0),
        "noise_sigma": jnp.clip(jnp.exp(jax.random.uniform(keys[4], (S,), jnp.float32, math.log(0.15), math.log(0.6))), 0.15, 0.6),
    }


diffusion_step = 0.06


def diffuse(padded, depth_padded):
    centre = depth_padded[1:-1, 1:-1]
    north_face = 0.5 * (centre + depth_padded[1:-1, 2:])
    south_face = 0.5 * (centre + depth_padded[1:-1, :-2])
    east_face = 0.5 * (centre + depth_padded[2:, 1:-1])
    west_face = 0.5 * (centre + depth_padded[:-2, 1:-1])
    middle = padded[:, 1:-1, 1:-1]
    face_flux = north_face * (padded[:, 1:-1, 2:] - middle)
    face_flux = face_flux + south_face * (padded[:, 1:-1, :-2] - middle)
    face_flux = face_flux + east_face * (padded[:, 2:, 1:-1] - middle)
    face_flux = face_flux + west_face * (padded[:, :-2, 1:-1] - middle)
    return middle + diffusion_step * face_flux


def reference(adjoint, seafloor_depth, sensor_row, sensor_column, noise_sigma):
    depth_padded = jnp.pad(seafloor_depth, 1)

    def smooth(sensor_block):
        current = sensor_block.astype(jnp.float32)
        for _ in range(SWEEPS):
            current = diffuse(jnp.pad(current, ((0, 0), (1, 1), (1, 1))), depth_padded)
        return current.astype(jnp.bfloat16)

    blocks = adjoint.reshape(N_GX, S // N_GX, NC, NR)
    smoothed = lax.map(smooth, blocks).reshape(S, NC * NR)
    partial_value = lax.dot_general(smoothed, smoothed, (((1,), (1,)), ((), ())), preferred_element_type=jnp.float32)
    gram = partial_value * (1.0 / (NC * NR))
    variance = noise_sigma * noise_sigma * seafloor_depth[sensor_column, sensor_row]
    operator = gram + jnp.diag(variance)
    spectral_bound = jnp.max(jnp.sum(jnp.abs(operator), axis=1))
    inverse = jnp.eye(S, dtype=jnp.float32) / spectral_bound
    for _ in range(ITERS):
        product = jnp.dot(inverse, operator, precision=lax.Precision.HIGHEST, preferred_element_type=jnp.float32)
        inverse = 2.0 * inverse - jnp.dot(product, inverse, precision=lax.Precision.HIGHEST, preferred_element_type=jnp.float32)
    gain_field = jnp.dot(inverse.astype(jnp.bfloat16), smoothed, preferred_element_type=jnp.float32)
    return gain_field.astype(jnp.bfloat16).reshape(S, NC, NR)
```

```python
import jax
import jax.numpy as jnp
from jax import lax
from jax.experimental import pallas as pl
from jax.experimental.pallas import tpu as pltpu
from jax.sharding import PartitionSpec as P

SWEEPS = 4
MESH = pl.DeviceIdType.MESH
LANES = 128
CLASSES = 3
CLASS_ROWS = 1024


diffusion_step = 0.06


def extended(block, sides, width):
    for axis, dim in sides:
        count = lax.axis_size(axis)
        forward = [(i, i + 1) for i in range(count - 1)]
        backward = [(target, source) for source, target in forward]
        low = lax.ppermute(
            lax.slice_in_dim(block, block.shape[dim] - width, None, axis=dim), axis, forward
        )
        high = lax.ppermute(lax.slice_in_dim(block, 0, width, axis=dim), axis, backward)
        block = jnp.concatenate([low, block, high], axis=dim)
    return block


def diffuse(padded, depth_padded):
    centre = depth_padded[1:-1, 1:-1]
    north_face = 0.5 * (centre + depth_padded[1:-1, 2:])
    south_face = 0.5 * (centre + depth_padded[1:-1, :-2])
    east_face = 0.5 * (centre + depth_padded[2:, 1:-1])
    west_face = 0.5 * (centre + depth_padded[:-2, 1:-1])
    middle = padded[:, 1:-1, 1:-1]
    face_flux = north_face * (padded[:, 1:-1, 2:] - middle)
    face_flux = face_flux + south_face * (padded[:, 1:-1, :-2] - middle)
    face_flux = face_flux + east_face * (padded[:, 2:, 1:-1] - middle)
    face_flux = face_flux + west_face * (padded[:, :-2, 1:-1] - middle)
    return middle + diffusion_step * face_flux


def position():
    gx, gy = lax.axis_index("gx"), lax.axis_index("gy")
    x, y, z, core = gy // 4, ((gy // 2) % 2) * 2 + gx // 4, gx % 4, gy % 2
    return [x, y, z], core


def device(place, core):
    x, y, z = place
    return ((y % 2) * 4 + z, x * 4 + (y // 2) * 2 + core)


def moved(place, axis, step):
    there = list(place)
    there[axis] = (place[axis] + step) % 4
    return there


def all_reduce_kernel(part, total, half_in, q_in, e_in, p_in, half, quarter, eighth, send, recv):
    place, core = position()
    barrier = pltpu.get_barrier_semaphore()
    pl.semaphore_signal(barrier, inc=1, device_id=device(place, 1 - core), device_id_type=MESH)
    for axis in range(3):
        for step in (1, 2, 3):
            pl.semaphore_signal(
                barrier, inc=1, device_id=device(moved(place, axis, step), core), device_id_type=MESH
            )
    pl.semaphore_wait(barrier, 10)

    def rows(start, size):
        return pl.ds(pl.multiple_of(start, 8), size)

    def push(src, dst, sem, place_to, core_to):
        copy = pltpu.make_async_remote_copy(
            src_ref=src,
            dst_ref=dst,
            send_sem=send.at[sem],
            recv_sem=recv.at[sem],
            device_id=device(place_to, core_to),
            device_id_type=MESH,
        )
        copy.start()
        return copy

    started = []
    pending = {}
    for q in range(CLASSES):
        copy = push(
            part.at[rows(q * CLASS_ROWS + (1 - core) * 512, 512)],
            half_in.at[q],
            q,
            place,
            1 - core,
        )
        pending[q, 0] = [copy]
    own = {}
    sizes = (512, 128, 32, 8)
    slots = (None, q_in, e_in, p_in)
    sums = (half, quarter, eighth)
    base = {q: q * CLASS_ROWS + core * 512 for q in range(CLASSES)}
    for stage in range(4):
        for q in range(CLASSES):
            for copy in pending[q, stage]:
                copy.wait_recv()
            started += pending[q, stage]
            size = sizes[stage]
            if stage == 0:
                value = part[rows(base[q], 512), :] + half_in[q]
            else:
                axis = (q + stage - 1) % 3
                value = sums[stage - 1][q, rows(place[axis] * size, size), :]
                for slot in range(3):
                    value = value + slots[stage][q, slot]
                base[q] = base[q] + place[axis] * size
            if stage == 3:
                total[rows(base[q], 8), :] = value
                continue
            sums[stage][q] = value
            axis = (q + stage) % 3
            size = sizes[stage + 1]
            pending[q, stage + 1] = [
                push(
                    sums[stage].at[q, rows(((place[axis] + step) % 4) * size, size)],
                    slots[stage + 1].at[q, step - 1],
                    3 + (stage * CLASSES + q) * 3 + step - 1,
                    moved(place, axis, step),
                    core,
                )
                for step in (1, 2, 3)
            ]
    sem0 = 3 + 27
    for stage in (3, 2, 1, 0):
        for q in range(CLASSES):
            if stage < 3:
                for copy in pending[q, "g", stage + 1]:
                    copy.wait_recv()
                started += pending[q, "g", stage + 1]
                axis = (q + stage) % 3
                base[q] = base[q] - place[axis] * sizes[stage + 1]
            size = sizes[stage]
            here = total.at[rows(base[q], size)]
            if stage == 0:
                pending[q, "g", 0] = [push(here, here, sem0 + 27 + q, place, 1 - core)]
                continue
            axis = (q + stage - 1) % 3
            pending[q, "g", stage] = [
                push(
                    here,
                    here,
                    sem0 + ((stage - 1) * CLASSES + q) * 3 + step - 1,
                    moved(place, axis, step),
                    core,
                )
                for step in (1, 2, 3)
            ]
    for q in range(CLASSES):
        for copy in pending[q, "g", 0]:
            copy.wait_recv()
        started += pending[q, "g", 0]
    for copy in started:
        copy.wait_send()


def all_reduced(part):
    vmem = pl.BlockSpec(memory_space=pltpu.VMEM)
    f32 = jnp.float32
    return pl.pallas_call(
        all_reduce_kernel,
        out_shape=jax.ShapeDtypeStruct(part.shape, f32),
        in_specs=[vmem],
        out_specs=vmem,
        scratch_shapes=[
            pltpu.VMEM((CLASSES, 512, LANES), f32),
            pltpu.VMEM((CLASSES, 3, 128, LANES), f32),
            pltpu.VMEM((CLASSES, 3, 32, LANES), f32),
            pltpu.VMEM((CLASSES, 3, 8, LANES), f32),
            pltpu.VMEM((CLASSES, 512, LANES), f32),
            pltpu.VMEM((CLASSES, 128, LANES), f32),
            pltpu.VMEM((CLASSES, 32, LANES), f32),
            pltpu.SemaphoreType.DMA((60,)),
            pltpu.SemaphoreType.DMA((60,)),
        ],
        compiler_params=pltpu.CompilerParams(collective_id=0, has_side_effects=True),
        name="gram_all_reduce",
    )(part)


def dot3(left, right):
    return jnp.dot(left, right, precision=lax.Precision.HIGH, preferred_element_type=jnp.float32)


def local(adjoint, seafloor_depth, sensor_row, sensor_column, noise_sigma):
    sensors, tile_columns, tile_rows = adjoint.shape
    column_offset = lax.axis_index("gy") * tile_columns
    row_offset = lax.axis_index("gx") * tile_rows
    pick_column = (
        sensor_column[:, None] - column_offset == jnp.arange(tile_columns)[None, :]
    ).astype(jnp.float32)
    pick_row = (sensor_row[:, None] - row_offset == jnp.arange(tile_rows)[None, :]).astype(
        jnp.float32
    )
    picked = jnp.sum(
        jnp.dot(pick_column, seafloor_depth, precision=lax.Precision.HIGHEST) * pick_row, axis=1
    )
    variance = noise_sigma * noise_sigma * picked
    depth_padded = extended(seafloor_depth, (("gx", 1), ("gy", 0)), SWEEPS)
    inside = (depth_padded > 0.0).astype(jnp.float32)
    padded = extended(adjoint, (("gx", 2), ("gy", 1)), SWEEPS).astype(jnp.float32)
    padded_columns, padded_rows = depth_padded.shape
    for sweep_index in range(SWEEPS):
        depth_view = depth_padded[
            sweep_index : padded_columns - sweep_index, sweep_index : padded_rows - sweep_index
        ]
        mask_view = inside[
            sweep_index + 1 : padded_columns - sweep_index - 1,
            sweep_index + 1 : padded_rows - sweep_index - 1,
        ]
        padded = diffuse(padded, depth_view) * mask_view
    smoothed = padded.astype(jnp.bfloat16).reshape(sensors, tile_columns * tile_rows)
    inverse_cells = 1.0 / (tile_columns * tile_rows * lax.axis_size("gx") * lax.axis_size("gy"))
    partial_value = lax.dot_general(
        smoothed, smoothed, (((1,), (1,)), ((), ())), preferred_element_type=jnp.float32
    )
    partial_value = partial_value * inverse_cells + jnp.diag(variance)
    blocks = -(-sensors // LANES)
    wide = jnp.pad(partial_value, ((0, 0), (0, blocks * LANES - sensors)))
    stacked = jnp.concatenate([wide[:, i * LANES : (i + 1) * LANES] for i in range(blocks)])
    stacked = jnp.pad(stacked, ((0, CLASSES * CLASS_ROWS - stacked.shape[0]), (0, 0)))
    stacked = all_reduced(stacked)
    operator = jnp.concatenate(
        [stacked[i * sensors : (i + 1) * sensors] for i in range(blocks)], axis=1
    )[:, :sensors]
    spectral_bound = jnp.max(jnp.sum(jnp.abs(operator), axis=1))
    identity = jnp.eye(sensors, dtype=jnp.float32)
    residual = identity - operator / spectral_bound
    inverse = (identity + residual) / spectral_bound
    for _ in range(3):
        residual = dot3(residual, residual)
        inverse = inverse + dot3(residual, inverse)
    gain_field = jnp.dot(inverse.astype(jnp.bfloat16), smoothed, preferred_element_type=jnp.float32)
    return gain_field.astype(jnp.bfloat16).reshape(sensors, tile_columns, tile_rows)


def solution(mesh):
    in_specs = (P(None, "gy", "gx"), P("gy", "gx"), P(), P(), P())
    out_specs = P(None, "gy", "gx")
    return jax.shard_map(local, mesh=mesh, in_specs=in_specs, out_specs=out_specs, check_vma=False)
```

```python
import jax
import jax.numpy as jnp
from jax import lax
from jax.experimental import pallas as pl
from jax.experimental.pallas import tpu as pltpu
from jax.sharding import PartitionSpec as P

SWEEPS = 4
MESH = pl.DeviceIdType.MESH
LANES = 128
CLASSES = 3
CLASS_ROWS = 1024


diffusion_step = 0.06


def position():
    gx, gy = lax.axis_index("gx"), lax.axis_index("gy")
    x, y, z, core = gy // 4, ((gy // 2) % 2) * 2 + gx // 4, gx % 4, gy % 2
    return [x, y, z], core


def device(place, core):
    x, y, z = place
    return ((y % 2) * 4 + z, x * 4 + (y // 2) * 2 + core)


def moved(place, axis, step):
    there = list(place)
    there[axis] = (place[axis] + step) % 4
    return there


def all_reduce_kernel(part, total, half_in, q_in, e_in, p_in, half, quarter, eighth, send, recv):
    place, core = position()
    barrier = pltpu.get_barrier_semaphore()
    pl.semaphore_signal(barrier, inc=1, device_id=device(place, 1 - core), device_id_type=MESH)
    for axis in range(3):
        for step in (1, 2, 3):
            pl.semaphore_signal(
                barrier, inc=1, device_id=device(moved(place, axis, step), core), device_id_type=MESH
            )
    pl.semaphore_wait(barrier, 10)

    def rows(start, size):
        return pl.ds(pl.multiple_of(start, 8), size)

    def push(src, dst, sem, place_to, core_to):
        copy = pltpu.make_async_remote_copy(
            src_ref=src,
            dst_ref=dst,
            send_sem=send.at[sem],
            recv_sem=recv.at[sem],
            device_id=device(place_to, core_to),
            device_id_type=MESH,
        )
        copy.start()
        return copy

    started = []
    pending = {}
    for q in range(CLASSES):
        copy = push(
            part.at[rows(q * CLASS_ROWS + (1 - core) * 512, 512)],
            half_in.at[q],
            q,
            place,
            1 - core,
        )
        pending[q, 0] = [copy]
    own = {}
    sizes = (512, 128, 32, 8)
    slots = (None, q_in, e_in, p_in)
    sums = (half, quarter, eighth)
    base = {q: q * CLASS_ROWS + core * 512 for q in range(CLASSES)}
    for stage in range(4):
        for q in range(CLASSES):
            for copy in pending[q, stage]:
                copy.wait_recv()
            started += pending[q, stage]
            size = sizes[stage]
            if stage == 0:
                value = part[rows(base[q], 512), :] + half_in[q]
            else:
                axis = (q + stage - 1) % 3
                value = sums[stage - 1][q, rows(place[axis] * size, size), :]
                for slot in range(3):
                    value = value + slots[stage][q, slot]
                base[q] = base[q] + place[axis] * size
            if stage == 3:
                total[rows(base[q], 8), :] = value
                continue
            sums[stage][q] = value
            axis = (q + stage) % 3
            size = sizes[stage + 1]
            pending[q, stage + 1] = [
                push(
                    sums[stage].at[q, rows(((place[axis] + step) % 4) * size, size)],
                    slots[stage + 1].at[q, step - 1],
                    3 + (stage * CLASSES + q) * 3 + step - 1,
                    moved(place, axis, step),
                    core,
                )
                for step in (1, 2, 3)
            ]
    sem0 = 3 + 27
    for stage in (3, 2, 1, 0):
        for q in range(CLASSES):
            if stage < 3:
                for copy in pending[q, "g", stage + 1]:
                    copy.wait_recv()
                started += pending[q, "g", stage + 1]
                axis = (q + stage) % 3
                base[q] = base[q] - place[axis] * sizes[stage + 1]
            size = sizes[stage]
            here = total.at[rows(base[q], size)]
            if stage == 0:
                pending[q, "g", 0] = [push(here, here, sem0 + 27 + q, place, 1 - core)]
                continue
            axis = (q + stage - 1) % 3
            pending[q, "g", stage] = [
                push(
                    here,
                    here,
                    sem0 + ((stage - 1) * CLASSES + q) * 3 + step - 1,
                    moved(place, axis, step),
                    core,
                )
                for step in (1, 2, 3)
            ]
    for q in range(CLASSES):
        for copy in pending[q, "g", 0]:
            copy.wait_recv()
        started += pending[q, "g", 0]
    for copy in started:
        copy.wait_send()


def all_reduced(part):
    vmem = pl.BlockSpec(memory_space=pltpu.VMEM)
    f32 = jnp.float32
    return pl.pallas_call(
        all_reduce_kernel,
        out_shape=jax.ShapeDtypeStruct(part.shape, f32),
        in_specs=[vmem],
        out_specs=vmem,
        scratch_shapes=[
            pltpu.VMEM((CLASSES, 512, LANES), f32),
            pltpu.VMEM((CLASSES, 3, 128, LANES), f32),
            pltpu.VMEM((CLASSES, 3, 32, LANES), f32),
            pltpu.VMEM((CLASSES, 3, 8, LANES), f32),
            pltpu.VMEM((CLASSES, 512, LANES), f32),
            pltpu.VMEM((CLASSES, 128, LANES), f32),
            pltpu.VMEM((CLASSES, 32, LANES), f32),
            pltpu.SemaphoreType.DMA((60,)),
            pltpu.SemaphoreType.DMA((60,)),
        ],
        compiler_params=pltpu.CompilerParams(collective_id=0, has_side_effects=True),
        name="gram_all_reduce",
    )(part)


def dot3(left, right):
    return jnp.dot(left, right, precision=lax.Precision.HIGH, preferred_element_type=jnp.float32)


SENSORS = 600
WIDE = 640
CHUNKS = WIDE // LANES
TOP = 16
BLOCK = 48
DIRECTIONS = ((0, 1), (0, -1), (1, 0), (-1, 0), (1, 1), (1, -1), (-1, 1), (-1, -1))


def smooth_kernel(
    field, depth, variance, smoothed, gram,
    level0, coefficient, levels, total, west, east, low_rows, high_rows, low_send, high_send,
    depths, send, recv,
):
    gx, gy = lax.axis_index("gx"), lax.axis_index("gy")
    columns, rows, _ = field.shape
    f32, bf16 = jnp.float32, jnp.bfloat16

    def neighbour(step):
        return (lax.rem(gx + step[0] + 8, 8), lax.rem(gy + step[1] + 16, 16))

    barrier = pltpu.get_barrier_semaphore()
    for step in DIRECTIONS:
        pl.semaphore_signal(barrier, inc=1, device_id=neighbour(step), device_id_type=MESH)

    upper = lax.broadcasted_iota(jnp.int32, (8, WIDE), 0) < 4

    def pack(group, _):
        first, last = [], []
        for pair in (0, 1):
            at = group * 4 + pair * 2
            a = field[at, pl.ds(0, 16), :].astype(f32)[:8]
            b = field[at + 1, pl.ds(0, 16), :].astype(f32)[:8]
            first.append(jnp.where(upper, a, pltpu.roll(b, 4, 0)))
            a = field[at, pl.ds(rows - 16, 16), :].astype(f32)[8:]
            b = field[at + 1, pl.ds(rows - 16, 16), :].astype(f32)[8:]
            last.append(jnp.where(upper, pltpu.roll(a, 4, 0), b))
        at = pl.ds(pl.multiple_of(group * 16, 16), 16)
        low_send[at, :] = jnp.concatenate(first).astype(bf16)
        high_send[at, :] = jnp.concatenate(last).astype(bf16)
        return 0

    lax.fori_loop(0, columns // 4, pack, 0)
    pl.semaphore_wait(barrier, 8)

    def push(src, dst, sem, step):
        copy = pltpu.make_async_remote_copy(
            src_ref=src,
            dst_ref=dst,
            send_sem=send.at[sem],
            recv_sem=recv.at[sem],
            device_id=neighbour(step),
            device_id_type=MESH,
        )
        copy.start()
        return copy

    n4 = columns * 4
    depth_copies = [push(depth, depths.at[k], k, DIRECTIONS[k]) for k in range(8)]
    halo_copies = [
        push(field.at[pl.ds(columns - 4, 4)], west, 8, (0, 1)),
        push(field.at[pl.ds(0, 4)], east, 9, (0, -1)),
        push(high_send, low_rows.at[pl.ds(16, n4)], 10, (1, 0)),
        push(low_send, high_rows.at[pl.ds(16, n4)], 11, (-1, 0)),
        push(high_send.at[pl.ds(n4 - 16, 16)], low_rows.at[pl.ds(0, 16)], 12, (1, 1)),
        push(high_send.at[pl.ds(0, 16)], low_rows.at[pl.ds(n4 + 16, 16)], 13, (1, -1)),
        push(low_send.at[pl.ds(n4 - 16, 16)], high_rows.at[pl.ds(0, 16)], 14, (-1, 1)),
        push(low_send.at[pl.ds(0, 16)], high_rows.at[pl.ds(n4 + 16, 16)], 15, (-1, -1)),
    ]

    def widen(src, at, to):
        for chunk in range(CHUNKS):
            level0[to, chunk, pl.ds(TOP, rows), :] = src[
                at, :, pl.ds(chunk * LANES, LANES)
            ].astype(f32)

    def fill(column, _):
        widen(field, column, column + 4)
        return 0

    lax.fori_loop(0, columns, fill, 0)

    for copy in depth_copies:
        copy.wait_recv()
    inside_x = {1: gx > 0, -1: gx < 7, 0: gx >= 0}
    inside_y = {1: gy > 0, -1: gy < 15, 0: gy >= 0}

    def tile(step):
        if step == (0, 0):
            return depth[...]
        keep = jnp.logical_and(inside_x[step[0]], inside_y[step[1]])
        return depths[DIRECTIONS.index(step)] * jnp.where(keep, 1.0, 0.0)

    turned = []
    for dx in (1, 0, -1):
        stack = jnp.concatenate(
            [
                tile((dx, 1))[columns - 8 :],
                tile((dx, 0)),
                tile((dx, -1))[:8],
                jnp.zeros((LANES - columns - 16, rows), f32),
            ]
        )
        turned.append(jnp.transpose(stack))
    here = jnp.concatenate([turned[0][rows - TOP :], turned[1], turned[2][:TOP]])
    height = rows + 2 * TOP
    others = (
        pltpu.roll(here, height - 1, 0),
        pltpu.roll(here, 1, 0),
        pltpu.roll(here, LANES - 1, 1),
        pltpu.roll(here, 1, 1),
    )
    weights = [diffusion_step * (0.5 * (here + other)) for other in others]
    kept = [jnp.where(other > 0.0, w, 0.0) for other, w in zip(others, weights)]
    centre = 1.0 - (weights[0] + weights[1] + weights[2] + weights[3])
    for index, value in enumerate([centre] + kept):
        value = value[8 : height - 8]
        for column in range(columns + 6):
            coefficient[index, column] = jnp.broadcast_to(
                value[:, column + 5 : column + 6], (height - 16, LANES)
            )

    for copy in halo_copies:
        copy.wait_recv()

    def edge(column, _):
        widen(west, column, column)
        widen(east, column, column + columns + 4)
        return 0

    lax.fori_loop(0, 4, edge, 0)

    def rims(group, _):
        at = pl.ds(pl.multiple_of(group * 16, 16), 16)
        low, high = low_rows[at, :].astype(f32), high_rows[at, :].astype(f32)
        for pair in (0, 1):
            for odd in (0, 1):
                a, b = low[pair * 8 : pair * 8 + 8], high[pair * 8 : pair * 8 + 8]
                if odd:
                    b = pltpu.roll(b, 4, 0)
                else:
                    a = pltpu.roll(a, 4, 0)
                for chunk in range(CHUNKS):
                    part = slice(chunk * LANES, (chunk + 1) * LANES)
                    column = group * 4 + pair * 2 + odd
                    level0[column, chunk, pl.ds(TOP - 8, 8), :] = a[:, part]
                    level0[column, chunk, pl.ds(TOP + rows, 8), :] = b[:, part]
        return 0

    lax.fori_loop(0, (columns + 8) // 4, rims, 0)

    def sweep(read, write, column, first, last):
        for start in range(first, last, BLOCK):
            size = min(BLOCK, last - start)
            k = [coefficient[index, column, pl.ds(8 + start, size), :] for index in range(5)]
            for chunk in range(CHUNKS):
                at = TOP + start
                write(
                    chunk,
                    start,
                    size,
                    k[0] * read(1, chunk, at, size)
                    + k[1] * read(1, chunk, at + 1, size)
                    + k[2] * read(1, chunk, at - 1, size)
                    + k[3] * read(2, chunk, at, size)
                    + k[4] * read(0, chunk, at, size),
                )

    def wave(i, _):
        slots = [lax.rem(i + 1, 3), lax.rem(i + 2, 3), lax.rem(i, 3)]

        def read_first(which, chunk, at, size):
            return level0[i + which, chunk, pl.ds(at, size), :]

        def read_level(level):
            return lambda which, chunk, at, size: levels[
                level, slots[which], chunk, pl.ds(at, size), :
            ]

        def write_level(level):
            def write(chunk, start, size, value):
                levels[level, slots[2], chunk, pl.ds(TOP + start, size), :] = value

            return write

        sweep(read_first, write_level(0), i, -8, rows + 8)
        sweep(read_level(0), write_level(1), jnp.maximum(i - 1, 0), -8, rows + 8)
        sweep(read_level(1), write_level(2), jnp.maximum(i - 2, 0), -8, rows + 8)

        @pl.when(i >= 6)
        def _():
            def write(chunk, start, size, value):
                smoothed[i - 6, pl.ds(start, size), pl.ds(chunk * LANES, LANES)] = value.astype(
                    bf16
                )

            sweep(read_level(2), write, i - 3, 0, rows)

        return 0

    lax.fori_loop(0, columns + 6, wave, 0)

    total[...] = jnp.zeros_like(total)

    def accumulate(group, _):
        part = smoothed[pl.ds(group * 8, 8)].reshape(8 * rows, WIDE)
        total[...] += lax.dot_general(
            part, part, (((0,), (0,)), ((), ())), preferred_element_type=f32
        )
        return 0

    lax.fori_loop(0, columns // 8, accumulate, 0)
    sensors = SENSORS
    inverse_cells = 1.0 / (columns * rows * 128)
    for chunk in range(CHUNKS):
        part = slice(chunk * LANES, (chunk + 1) * LANES)
        row = lax.broadcasted_iota(jnp.int32, (sensors, LANES), 0)
        lane = lax.broadcasted_iota(jnp.int32, (sensors, LANES), 1) + chunk * LANES
        gram[pl.ds(chunk * sensors, sensors), :] = total[:sensors, part] * inverse_cells + jnp.where(
            row == lane, variance[:, part], 0.0
        )
    gram[pl.ds(CHUNKS * sensors, gram.shape[0] - CHUNKS * sensors), :] = jnp.zeros(
        (gram.shape[0] - CHUNKS * sensors, LANES), f32
    )
    for copy in depth_copies + halo_copies:
        copy.wait_send()


def smoothed_and_gram(field, depth, variance):
    vmem = pl.BlockSpec(memory_space=pltpu.VMEM)
    f32, bf16 = jnp.float32, jnp.bfloat16
    columns, rows, _ = field.shape
    height = rows + 2 * TOP
    rim = pltpu.VMEM(((columns + 8) * 4, WIDE), bf16)
    return pl.pallas_call(
        smooth_kernel,
        out_shape=(
            jax.ShapeDtypeStruct(field.shape, bf16),
            jax.ShapeDtypeStruct((CLASSES * CLASS_ROWS, LANES), f32),
        ),
        in_specs=[vmem] * 3,
        out_specs=(vmem, vmem),
        scratch_shapes=[
            pltpu.VMEM((columns + 8, CHUNKS, height, LANES), f32),
            pltpu.VMEM((5, columns + 6, height - 16, LANES), f32),
            pltpu.VMEM((3, 3, CHUNKS, height, LANES), f32),
            pltpu.VMEM((WIDE, WIDE), f32),
            pltpu.VMEM((4, rows, WIDE), bf16),
            pltpu.VMEM((4, rows, WIDE), bf16),
            rim,
            rim,
            pltpu.VMEM((columns * 4, WIDE), bf16),
            pltpu.VMEM((columns * 4, WIDE), bf16),
            pltpu.VMEM((8, columns, rows), f32),
            pltpu.SemaphoreType.DMA((16,)),
            pltpu.SemaphoreType.DMA((16,)),
        ],
        compiler_params=pltpu.CompilerParams(
            collective_id=1, has_side_effects=True, vmem_limit_bytes=66_000_000
        ),
        name="smooth_and_gram",
    )(field, depth, variance)


def local(adjoint, seafloor_depth, sensor_row, sensor_column, noise_sigma):
    sensors, tile_columns, tile_rows = adjoint.shape
    column_offset = lax.axis_index("gy") * tile_columns
    row_offset = lax.axis_index("gx") * tile_rows
    pick_column = (
        sensor_column[:, None] - column_offset == jnp.arange(tile_columns)[None, :]
    ).astype(jnp.float32)
    pick_row = (sensor_row[:, None] - row_offset == jnp.arange(tile_rows)[None, :]).astype(
        jnp.float32
    )
    picked = jnp.sum(
        jnp.dot(pick_column, seafloor_depth, precision=lax.Precision.HIGHEST) * pick_row, axis=1
    )
    variance = noise_sigma * noise_sigma * picked
    variance = jnp.pad(variance, (0, WIDE - sensors)).reshape(1, WIDE)
    field = jnp.pad(jnp.transpose(adjoint, (1, 2, 0)), ((0, 0), (0, 0), (0, WIDE - sensors)))
    smoothed, stacked = smoothed_and_gram(field, seafloor_depth, variance)
    stacked = all_reduced(stacked)
    operator = jnp.concatenate(
        [stacked[i * sensors : (i + 1) * sensors] for i in range(CHUNKS)], axis=1
    )[:, :sensors]
    spectral_bound = jnp.max(jnp.sum(jnp.abs(operator), axis=1))
    identity = jnp.eye(sensors, dtype=jnp.float32)
    residual = identity - operator / spectral_bound
    inverse = (identity + residual) / spectral_bound
    for _ in range(3):
        residual = dot3(residual, residual)
        inverse = inverse + dot3(residual, inverse)
    inverse = jnp.pad(inverse.astype(jnp.bfloat16), ((0, 0), (0, WIDE - sensors)))
    gain_field = lax.dot_general(
        inverse, smoothed, (((1,), (2,)), ((), ())), preferred_element_type=jnp.float32
    )
    return gain_field.astype(jnp.bfloat16)


def solution(mesh):
    in_specs = (P(None, "gy", "gx"), P("gy", "gx"), P(), P(), P())
    out_specs = P(None, "gy", "gx")
    return jax.shard_map(local, mesh=mesh, in_specs=in_specs, out_specs=out_specs, check_vma=False)
```

```python
import jax
import jax.numpy as jnp
from jax import lax
from jax.experimental import pallas as pl
from jax.experimental.pallas import tpu as pltpu
from jax.sharding import PartitionSpec as P

SWEEPS = 4
MESH = pl.DeviceIdType.MESH
LANES = 128
CLASSES = 3
CLASS_ROWS = 768


diffusion_step = 0.06


def position():
    gx, gy = lax.axis_index("gx"), lax.axis_index("gy")
    x, y, z, core = gy // 4, ((gy // 2) % 2) * 2 + gx // 4, gx % 4, gy % 2
    return [x, y, z], core


def device(place, core):
    x, y, z = place
    return ((y % 2) * 4 + z, x * 4 + (y // 2) * 2 + core)


def moved(place, axis, step):
    there = list(place)
    there[axis] = (place[axis] + step) % 4
    return there


def all_reduce_kernel(part, total, half_in, q_in, e_in, p_in, half, quarter, send, recv):
    place, core = position()
    barrier = pltpu.get_barrier_semaphore()
    pl.semaphore_signal(barrier, inc=1, device_id=device(place, 1 - core), device_id_type=MESH)
    for axis in range(3):
        for step in (1, 2, 3):
            pl.semaphore_signal(
                barrier, inc=1, device_id=device(moved(place, axis, step), core), device_id_type=MESH
            )
    pl.semaphore_wait(barrier, 10)

    def rows(start, size):
        return pl.ds(pl.multiple_of(start, 8), size)

    def push(src, dst, sem, place_to, core_to):
        copy = pltpu.make_async_remote_copy(
            src_ref=src,
            dst_ref=dst,
            send_sem=send.at[sem],
            recv_sem=recv.at[sem],
            device_id=device(place_to, core_to),
            device_id_type=MESH,
        )
        copy.start()
        return copy

    sizes = (CLASS_ROWS // 2, CLASS_ROWS // 8, CLASS_ROWS // 32)
    started = []
    pending = {}
    for q in range(CLASSES):
        copy = push(
            part.at[rows(q * CLASS_ROWS + (1 - core) * sizes[0], sizes[0])],
            half_in.at[q],
            q,
            place,
            1 - core,
        )
        pending[q, 0] = [copy]
    slots = (None, q_in, e_in)
    sums = (half, quarter)
    base = {q: q * CLASS_ROWS + core * sizes[0] for q in range(CLASSES)}
    for stage in range(3):
        for q in range(CLASSES):
            for copy in pending[q, stage]:
                copy.wait_recv()
            started += pending[q, stage]
            size = sizes[stage]
            if stage == 0:
                value = part[rows(base[q], size), :] + half_in[q]
            else:
                axis = (q + stage - 1) % 3
                value = sums[stage - 1][q, rows(place[axis] * size, size), :]
                for slot in range(3):
                    value = value + slots[stage][q, slot]
                base[q] = base[q] + place[axis] * size
            axis = (q + stage) % 3
            if stage < 2:
                sums[stage][q] = value
                size = sizes[stage + 1]
                pending[q, stage + 1] = [
                    push(
                        sums[stage].at[q, rows(((place[axis] + step) % 4) * size, size)],
                        slots[stage + 1].at[q, step - 1],
                        3 + (stage * CLASSES + q) * 3 + step - 1,
                        moved(place, axis, step),
                        core,
                    )
                    for step in (1, 2, 3)
                ]
            else:
                mine = p_in.at[q, place[axis]]
                p_in[q, place[axis]] = value
                pending[q, 3] = [
                    push(
                        mine,
                        mine,
                        3 + (stage * CLASSES + q) * 3 + step - 1,
                        moved(place, axis, step),
                        core,
                    )
                    for step in (1, 2, 3)
                ]
    for q in range(CLASSES):
        for copy in pending[q, 3]:
            copy.wait_recv()
        started += pending[q, 3]
        value = (p_in[q, 0] + p_in[q, 1]) + (p_in[q, 2] + p_in[q, 3])
        total[rows(base[q], sizes[2]), :] = value
    sem0 = 3 + 27
    for stage in (2, 1, 0):
        for q in range(CLASSES):
            if stage < 2:
                for copy in pending[q, "g", stage + 1]:
                    copy.wait_recv()
                started += pending[q, "g", stage + 1]
                axis = (q + stage) % 3
                base[q] = base[q] - place[axis] * sizes[stage + 1]
            size = sizes[stage]
            here = total.at[rows(base[q], size)]
            if stage == 0:
                pending[q, "g", 0] = [push(here, here, sem0 + 27 + q, place, 1 - core)]
                continue
            axis = (q + stage - 1) % 3
            pending[q, "g", stage] = [
                push(
                    here,
                    here,
                    sem0 + ((stage - 1) * CLASSES + q) * 3 + step - 1,
                    moved(place, axis, step),
                    core,
                )
                for step in (1, 2, 3)
            ]
    for q in range(CLASSES):
        for copy in pending[q, "g", 0]:
            copy.wait_recv()
        started += pending[q, "g", 0]
    for copy in started:
        copy.wait_send()


def all_reduced(part):
    vmem = pl.BlockSpec(memory_space=pltpu.VMEM)
    f32 = jnp.float32
    return pl.pallas_call(
        all_reduce_kernel,
        out_shape=jax.ShapeDtypeStruct(part.shape, f32),
        in_specs=[vmem],
        out_specs=vmem,
        scratch_shapes=[
            pltpu.VMEM((CLASSES, CLASS_ROWS // 2, LANES), f32),
            pltpu.VMEM((CLASSES, 3, CLASS_ROWS // 8, LANES), f32),
            pltpu.VMEM((CLASSES, 3, CLASS_ROWS // 32, LANES), f32),
            pltpu.VMEM((CLASSES, 4, CLASS_ROWS // 32, LANES), f32),
            pltpu.VMEM((CLASSES, CLASS_ROWS // 2, LANES), f32),
            pltpu.VMEM((CLASSES, CLASS_ROWS // 8, LANES), f32),
            pltpu.SemaphoreType.DMA((60,)),
            pltpu.SemaphoreType.DMA((60,)),
        ],
        compiler_params=pltpu.CompilerParams(collective_id=0, has_side_effects=True),
        name="gram_all_reduce",
    )(part)


SENSORS = 600
WIDE = 640
CHUNKS = WIDE // LANES
BLOCKS = [(i, j) for i in range(CHUNKS) for j in range(i, CHUNKS)]
TOP = 16
BLOCK = 48
DIRECTIONS = ((0, 1), (0, -1), (1, 0), (-1, 0), (1, 1), (1, -1), (-1, 1), (-1, -1))


def smooth_kernel(
    adjoint, depth, sensor_row, sensor_column, noise, smoothed_out, gram,
    smoothed, level0, coefficient, levels, total, natural, west, east, low_rows, high_rows,
    low_send, high_send, edge_send, depths, send, recv, load_sem, out_sem,
):
    gx, gy = lax.axis_index("gx"), lax.axis_index("gy")
    sensors, columns, rows = adjoint.shape
    f32, bf16 = jnp.float32, jnp.bfloat16
    loads = []
    for chunk in range(CHUNKS):
        count = min(LANES, sensors - chunk * LANES)
        loads.append(
            pltpu.make_async_copy(
                adjoint.at[pl.ds(chunk * LANES, count)],
                natural.at[chunk, pl.ds(0, count)],
                load_sem.at[chunk],
            )
        )
        loads[-1].start()
    spare = CHUNKS * LANES - sensors
    natural[CHUNKS - 1, pl.ds(LANES - spare, spare)] = jnp.zeros((spare, columns, rows), bf16)

    def neighbour(step):
        return (lax.rem(gx + step[0] + 8, 8), lax.rem(gy + step[1] + 16, 16))

    barrier = pltpu.get_barrier_semaphore()
    for step in DIRECTIONS:
        pl.semaphore_signal(barrier, inc=1, device_id=neighbour(step), device_id_type=MESH)

    upper = lax.broadcasted_iota(jnp.int32, (8, LANES), 0) < 4

    def turn(chunk, half):
        part = natural[chunk, :, pl.ds(pl.multiple_of(half * 16, 16), 16), :]
        level0[pl.ds(half * 16 + 4, 16), chunk, pl.ds(TOP, rows), :] = jnp.transpose(
            part.astype(f32), (1, 2, 0)
        )

    def pack(chunk, group):
        first, last = [], []
        for pair in (0, 1):
            at = group * 4 + pair * 2 + 4
            a, b = [level0[at + odd, chunk, pl.ds(TOP, 8), :] for odd in (0, 1)]
            first.append(jnp.where(upper, a, pltpu.roll(b, 4, 0)))
            a, b = [level0[at + odd, chunk, pl.ds(TOP + rows - 8, 8), :] for odd in (0, 1)]
            last.append(jnp.where(upper, pltpu.roll(a, 4, 0), b))
        at = pl.ds(pl.multiple_of(group * 16, 16), 16)
        low_send[chunk, at, :] = jnp.concatenate(first).astype(bf16)
        high_send[chunk, at, :] = jnp.concatenate(last).astype(bf16)

    def push(src, dst, sem, step):
        copy = pltpu.make_async_remote_copy(
            src_ref=src,
            dst_ref=dst,
            send_sem=send.at[sem],
            recv_sem=recv.at[sem],
            device_id=neighbour(step),
            device_id_type=MESH,
        )
        copy.start()
        return copy

    n4 = columns * 4
    row_copies = []
    depth_copies = []
    for chunk in range(CHUNKS):
        loads[chunk].wait()
        lax.fori_loop(0, columns // 16, lambda half, _: (turn(chunk, half), 0)[1], 0)
        lax.fori_loop(0, columns // 4, lambda group, _: (pack(chunk, group), 0)[1], 0)
        if chunk == 0:
            pl.semaphore_wait(barrier, 8)
            depth_copies = [push(depth, depths.at[k], k, DIRECTIONS[k]) for k in range(8)]
        inner = pl.ds(16, n4)
        row_copies += [
            push(high_send.at[chunk], low_rows.at[chunk, inner], 14 + chunk, (1, 0)),
            push(low_send.at[chunk], high_rows.at[chunk, inner], 19 + chunk, (-1, 0)),
        ]

    def edges(column, _):
        edge_send[column] = level0[column + 4, :, pl.ds(TOP, rows), :].astype(bf16)
        edge_send[column + 4] = level0[column + columns, :, pl.ds(TOP, rows), :].astype(bf16)
        return 0

    lax.fori_loop(0, 4, edges, 0)
    front, back = pl.ds(0, 16), pl.ds(n4 + 16, 16)
    final = pl.ds(n4 - 16, 16)
    halo_copies = [
        push(edge_send.at[pl.ds(4, 4)], west, 8, (0, 1)),
        push(edge_send.at[pl.ds(0, 4)], east, 9, (0, -1)),
        push(high_send.at[:, final], low_rows.at[:, front], 10, (1, 1)),
        push(high_send.at[:, front], low_rows.at[:, back], 11, (1, -1)),
        push(low_send.at[:, final], high_rows.at[:, front], 12, (-1, 1)),
        push(low_send.at[:, front], high_rows.at[:, back], 13, (-1, -1)),
    ]

    site_column = sensor_column[...].reshape(1, sensors) - gy * columns
    site_row = sensor_row[...].reshape(1, sensors) - gx * rows
    sigma = noise[...].reshape(1, sensors)
    pick = lax.broadcasted_iota(jnp.int32, (columns, sensors), 0) == site_column
    along = lax.dot_general(
        depth[...],
        pick.astype(f32),
        (((0,), (0,)), ((), ())),
        precision=lax.Precision.HIGHEST,
        preferred_element_type=f32,
    )
    pick = lax.broadcasted_iota(jnp.int32, (rows, sensors), 0) == site_row
    variance = sigma * sigma * jnp.sum(jnp.where(pick, along, 0.0), axis=0, keepdims=True)
    variance = jnp.concatenate([variance, jnp.zeros((1, spare), f32)], axis=1)

    for copy in depth_copies:
        copy.wait_recv()
    inside_x = {1: gx > 0, -1: gx < 7, 0: gx >= 0}
    inside_y = {1: gy > 0, -1: gy < 15, 0: gy >= 0}

    def tile(step):
        if step == (0, 0):
            return depth[...]
        keep = jnp.logical_and(inside_x[step[0]], inside_y[step[1]])
        return depths[DIRECTIONS.index(step)] * jnp.where(keep, 1.0, 0.0)

    turned = []
    for dx in (1, 0, -1):
        stack = jnp.concatenate(
            [
                tile((dx, 1))[columns - 8 :],
                tile((dx, 0)),
                tile((dx, -1))[:8],
                jnp.zeros((LANES - columns - 16, rows), f32),
            ]
        )
        turned.append(jnp.transpose(stack))
    here = jnp.concatenate([turned[0][rows - TOP :], turned[1], turned[2][:TOP]])
    height = rows + 2 * TOP
    others = (
        pltpu.roll(here, height - 1, 0),
        pltpu.roll(here, 1, 0),
        pltpu.roll(here, LANES - 1, 1),
        pltpu.roll(here, 1, 1),
    )
    weights = [diffusion_step * (0.5 * (here + other)) for other in others]
    kept = [jnp.where(other > 0.0, w, 0.0) for other, w in zip(others, weights)]
    centre = 1.0 - (weights[0] + weights[1] + weights[2] + weights[3])
    for index, value in enumerate([centre] + kept):
        value = value[8 : height - 8]
        for column in range(columns + 6):
            coefficient[index, column] = jnp.broadcast_to(
                value[:, column + 5 : column + 6], (height - 16, LANES)
            )

    def edge(column, _):
        level0[column, :, pl.ds(TOP, rows), :] = west[column].astype(f32)
        level0[column + columns + 4, :, pl.ds(TOP, rows), :] = east[column].astype(f32)
        return 0

    def rims(group, _):
        at = pl.ds(pl.multiple_of(group * 16, 16), 16)
        for chunk in range(CHUNKS):
            low, high = low_rows[chunk, at, :].astype(f32), high_rows[chunk, at, :].astype(f32)
            for pair in (0, 1):
                a, b = low[pair * 8 : pair * 8 + 8], high[pair * 8 : pair * 8 + 8]
                column = group * 4 + pair * 2
                before, after = pl.ds(TOP - 8, 8), pl.ds(TOP + rows, 8)
                level0[column, chunk, before, :] = pltpu.roll(a, 4, 0)
                level0[column + 1, chunk, before, :] = a
                level0[column, chunk, after, :] = b
                level0[column + 1, chunk, after, :] = pltpu.roll(b, 4, 0)
        return 0

    for copy in row_copies:
        copy.wait_recv()
    lax.fori_loop(1, columns // 4 + 1, rims, 0)

    def sweep(read, write, column, first, last):
        for start in range(first, last, BLOCK):
            size = min(BLOCK, last - start)
            k = [coefficient[index, column, pl.ds(8 + start, size), :] for index in range(5)]
            for chunk in range(CHUNKS):
                at = TOP + start
                write(
                    chunk,
                    start,
                    size,
                    k[0] * read(1, chunk, at, size)
                    + k[1] * read(1, chunk, at + 1, size)
                    + k[2] * read(1, chunk, at - 1, size)
                    + k[3] * read(2, chunk, at, size)
                    + k[4] * read(0, chunk, at, size),
                )

    up = columns + 2

    def wave(t, _):
        @pl.when(t == up - 4)
        def _():
            for copy in halo_copies:
                copy.wait_recv()
            lax.fori_loop(0, 4, edge, 0)
            rims(0, 0)
            rims(columns // 4 + 1, 0)

        down = (t >= up).astype(jnp.int32)
        sign = 1 - 2 * down
        first = jnp.where(t >= up, up - t, t + 1)
        order = jnp.where(t >= up, t - up + 2, t + 1)
        near, middle, far = [lax.rem(order + k, 3) for k in (0, 2, 1)]
        slots = (jnp.where(t >= up, near, far), middle, jnp.where(t >= up, far, near))

        def read_first(which, chunk, at, size):
            return level0[first + 3 + which, chunk, pl.ds(at, size), :]

        def read_level(level):
            return lambda which, chunk, at, size: levels[
                down, level, slots[which], chunk, pl.ds(at, size), :
            ]

        def write_level(level):
            def write(chunk, start, size, value):
                levels[down, level, near, chunk, pl.ds(TOP + start, size), :] = value

            return write

        sweep(read_first, write_level(0), first + 3, -8, rows + 8)
        sweep(read_level(0), write_level(1), first + 3 - sign, -8, rows + 8)
        sweep(read_level(1), write_level(2), first + 3 - 2 * sign, -8, rows + 8)

        @pl.when(t < 6)
        def _():
            level = lax.div(t, 2)
            levels[1, level, lax.rem(t + 1, 2)] = levels[0, level, near]

        @pl.when(t >= 6)
        def _():
            def write(chunk, start, size, value):
                smoothed[
                    first - 3 * sign, pl.ds(start, size), pl.ds(chunk * LANES, LANES)
                ] = value.astype(bf16)

            sweep(read_level(2), write, first + 3 - 3 * sign, 0, rows)

        return 0

    lax.fori_loop(0, up + 4, wave, 0)
    out_copy = pltpu.make_async_copy(smoothed, smoothed_out, out_sem)
    out_copy.start()

    total[...] = jnp.zeros_like(total)

    def accumulate(group, _):
        part = smoothed[pl.ds(group * 8, 8)].reshape(8 * rows, WIDE)
        for chunk in range(CHUNKS):
            at = chunk * LANES
            total[pl.ds(at, LANES), pl.ds(at, WIDE - at)] += lax.dot_general(
                part[:, at : at + LANES],
                part[:, at:],
                (((0,), (0,)), ((), ())),
                preferred_element_type=f32,
            )
        return 0

    lax.fori_loop(0, columns // 8, accumulate, 0)
    inverse_cells = 1.0 / (columns * rows * 128)
    diagonal = lax.broadcasted_iota(jnp.int32, (LANES, LANES), 0) == lax.broadcasted_iota(
        jnp.int32, (LANES, LANES), 1
    )
    for at, (i, j) in enumerate(BLOCKS):
        value = total[pl.ds(i * LANES, LANES), pl.ds(j * LANES, LANES)] * inverse_cells
        if i == j:
            part = slice(i * LANES, (i + 1) * LANES)
            value = value + jnp.where(diagonal, variance[:, part], 0.0)
        gram[pl.ds(at * LANES, LANES), :] = value
    unused = gram.shape[0] - len(BLOCKS) * LANES
    gram[pl.ds(len(BLOCKS) * LANES, unused), :] = jnp.zeros((unused, LANES), f32)
    out_copy.wait()
    for copy in depth_copies + row_copies + halo_copies:
        copy.wait_send()


def smoothed_and_gram(adjoint, depth, sensor_row, sensor_column, noise):
    vmem = pl.BlockSpec(memory_space=pltpu.VMEM)
    whole = pl.BlockSpec(memory_space=pl.ANY)
    f32, bf16 = jnp.float32, jnp.bfloat16
    _, columns, rows = adjoint.shape
    height = rows + 2 * TOP
    rim = pltpu.VMEM((CHUNKS, (columns + 8) * 4, LANES), bf16)
    return pl.pallas_call(
        smooth_kernel,
        out_shape=(
            jax.ShapeDtypeStruct((columns, rows, WIDE), bf16),
            jax.ShapeDtypeStruct((CLASSES * CLASS_ROWS, LANES), f32),
        ),
        in_specs=[whole] + [vmem] * 4,
        out_specs=(whole, vmem),
        scratch_shapes=[
            pltpu.VMEM((columns, rows, WIDE), bf16),
            pltpu.VMEM((columns + 8, CHUNKS, height, LANES), f32),
            pltpu.VMEM((5, columns + 6, height - 16, LANES), f32),
            pltpu.VMEM((2, 3, 3, CHUNKS, height, LANES), f32),
            pltpu.VMEM((WIDE, WIDE), f32),
            pltpu.VMEM((CHUNKS, LANES, columns, rows), bf16),
            pltpu.VMEM((4, CHUNKS, rows, LANES), bf16),
            pltpu.VMEM((4, CHUNKS, rows, LANES), bf16),
            rim,
            rim,
            pltpu.VMEM((CHUNKS, columns * 4, LANES), bf16),
            pltpu.VMEM((CHUNKS, columns * 4, LANES), bf16),
            pltpu.VMEM((8, CHUNKS, rows, LANES), bf16),
            pltpu.VMEM((8, columns, rows), f32),
            pltpu.SemaphoreType.DMA((24,)),
            pltpu.SemaphoreType.DMA((24,)),
            pltpu.SemaphoreType.DMA((CHUNKS,)),
            pltpu.SemaphoreType.DMA,
        ],
        compiler_params=pltpu.CompilerParams(
            collective_id=1, has_side_effects=True, vmem_limit_bytes=66_000_000
        ),
        name="smooth_and_gram",
    )(adjoint, depth, sensor_row, sensor_column, noise)


GROUP = 16


def split(value):
    high = value.astype(jnp.bfloat16)
    return high, (value - high.astype(jnp.float32)).astype(jnp.bfloat16)


def gain_kernel(stacked, smoothed_in, out, left, right, plane, smoothed, spread, ready, sems):
    f32, bf16 = jnp.float32, jnp.bfloat16
    columns, rows, _ = smoothed.shape
    load = pltpu.make_async_copy(smoothed_in, smoothed, sems.at[2])
    load.start()
    whole = plane.at[1]
    for at, (i, j) in enumerate(BLOCKS):
        block = stacked[pl.ds(at * LANES, LANES), :]
        size = min(LANES, SENSORS - i * LANES)
        whole[pl.ds(i * LANES, size), pl.ds(j * LANES, LANES)] = block[:size]
        if i != j:
            size = min(LANES, SENSORS - j * LANES)
            whole[pl.ds(j * LANES, size), pl.ds(i * LANES, LANES)] = jnp.transpose(block)[:size]
    blocks = [whole[:, chunk * LANES : (chunk + 1) * LANES] for chunk in range(CHUNKS)]
    reach = sum(jnp.sum(jnp.abs(block), axis=1, keepdims=True) for block in blocks)
    scale = 1.0 / jnp.max(reach)
    row = lax.broadcasted_iota(jnp.int32, (SENSORS, LANES), 0)
    lane = lax.broadcasted_iota(jnp.int32, (SENSORS, LANES), 1)
    zeros = jnp.zeros((WIDE - SENSORS, WIDE), bf16)

    def store(at, high, low):
        right[pl.ds(0, SENSORS), at] = high
        right[pl.ds(WIDE, SENSORS), at] = high
        right[pl.ds(2 * WIDE, SENSORS), at] = low

    for k in range(3):
        for half in range(2):
            right[pl.ds(k * WIDE + SENSORS, WIDE - SENSORS), pl.ds(half * WIDE, WIDE)] = zeros
    inverse = plane.at[1]
    for chunk, block in enumerate(blocks):
        diagonal = jnp.where(row == lane + chunk * LANES, 1.0, 0.0)
        residual = diagonal - block * scale
        at = pl.ds(chunk * LANES, LANES)
        plane[0, :, at] = residual
        inverse[:, at] = (diagonal + residual) * scale

    def product(width):
        value = plane[0]
        high, low = split(value)
        left[:, pl.ds(0, WIDE)] = high
        left[:, pl.ds(WIDE, WIDE)] = low
        left[:, pl.ds(2 * WIDE, WIDE)] = high
        store(pl.ds(0, WIDE), high, low)
        if width > WIDE:
            high, low = split(inverse[...])
            store(pl.ds(WIDE, WIDE), high, low)
        return jnp.dot(left[...], right[:, pl.ds(0, width)], preferred_element_type=f32)

    plane[0] = product(WIDE)
    for _ in range(2):
        both = product(2 * WIDE)
        plane[0] = both[:, :WIDE]
        inverse[...] = inverse[...] + both[:, WIDE:]
    high, low = split(plane[0])
    left[:, pl.ds(0, WIDE)] = high
    left[:, pl.ds(WIDE, WIDE)] = low
    left[:, pl.ds(2 * WIDE, WIDE)] = high
    high, low = split(inverse[...])
    store(pl.ds(0, WIDE), high, low)
    final = inverse[...] + jnp.dot(
        left[...], right[:, pl.ds(0, WIDE)], preferred_element_type=f32
    )
    left[:, pl.ds(0, WIDE)] = final.astype(bf16)

    load.wait()
    stores = []
    for group in range(columns // GROUP):
        for pair in range(GROUP // 2):
            field = smoothed[pl.ds(group * GROUP + pair * 2, 2)].reshape(2 * rows, WIDE)
            value = lax.dot_general(
                left[:, pl.ds(0, WIDE)],
                field,
                (((1,), (1,)), ((), ())),
                preferred_element_type=f32,
            )
            for odd in (0, 1):
                spread[pl.ds(pair * 2 + odd, SENSORS, stride=GROUP), :] = value[
                    :, odd * rows : (odd + 1) * rows
                ]
        ready[group] = spread[...].reshape(SENSORS, GROUP, rows).astype(bf16)
        stores.append(
            pltpu.make_async_copy(
                ready.at[group], out.at[:, pl.ds(group * GROUP, GROUP), :], sems.at[group]
            )
        )
        stores[-1].start()
    for store in stores:
        store.wait()


def gains(stacked, smoothed):
    vmem = pl.BlockSpec(memory_space=pltpu.VMEM)
    columns, rows, _ = smoothed.shape
    return pl.pallas_call(
        gain_kernel,
        out_shape=jax.ShapeDtypeStruct((SENSORS, columns, rows), jnp.bfloat16),
        in_specs=[vmem, pl.BlockSpec(memory_space=pl.ANY)],
        out_specs=pl.BlockSpec(memory_space=pl.ANY),
        scratch_shapes=[
            pltpu.VMEM((SENSORS, 3 * WIDE), jnp.bfloat16),
            pltpu.VMEM((3 * WIDE, 2 * WIDE), jnp.bfloat16),
            pltpu.VMEM((2, SENSORS, WIDE), jnp.float32),
            pltpu.VMEM(smoothed.shape, jnp.bfloat16),
            pltpu.VMEM((SENSORS * GROUP, LANES), jnp.float32),
            pltpu.VMEM((columns // GROUP, SENSORS, GROUP, rows), jnp.bfloat16),
            pltpu.SemaphoreType.DMA((3,)),
        ],
        compiler_params=pltpu.CompilerParams(vmem_limit_bytes=66_000_000),
        name="inverse_and_gain",
    )(stacked, smoothed)


def local(adjoint, seafloor_depth, sensor_row, sensor_column, noise_sigma):
    smoothed, stacked = smoothed_and_gram(
        adjoint, seafloor_depth, sensor_row, sensor_column, noise_sigma
    )
    return gains(all_reduced(stacked), smoothed)


def solution(mesh):
    in_specs = (P(None, "gy", "gx"), P("gy", "gx"), P(), P(), P())
    out_specs = P(None, "gy", "gx")
    return jax.shard_map(local, mesh=mesh, in_specs=in_specs, out_specs=out_specs, check_vma=False)
```

```python
import jax
import jax.numpy as jnp
from jax import lax
from jax.experimental import pallas as pl
from jax.experimental.pallas import tpu as pltpu
from jax.sharding import PartitionSpec as P

SWEEPS = 4
MESH = pl.DeviceIdType.MESH
LANES = 128
CLASSES = 3
CLASS_ROWS = 768


diffusion_step = 0.06


def position():
    gx, gy = lax.axis_index("gx"), lax.axis_index("gy")
    x, y, z, core = gy // 4, ((gy // 2) % 2) * 2 + gx // 4, gx % 4, gy % 2
    return [x, y, z], core


def device(place, core):
    x, y, z = place
    return ((y % 2) * 4 + z, x * 4 + (y // 2) * 2 + core)


def moved(place, axis, step):
    there = list(place)
    there[axis] = (place[axis] + step) % 4
    return there


def greet(barrier, place, core):
    pl.semaphore_signal(barrier, inc=1, device_id=device(place, 1 - core), device_id_type=MESH)
    for axis in range(3):
        for step in (1, 2, 3):
            pl.semaphore_signal(
                barrier, inc=1, device_id=device(moved(place, axis, step), core), device_id_type=MESH
            )


def all_reduce(part, total, half_in, q_in, e_in, p_in, half, quarter, send, recv):
    place, core = position()
    size0, size1, size2 = CLASS_ROWS // 2, CLASS_ROWS // 8, CLASS_ROWS // 32
    classes = range(CLASSES)

    def rows(start, size):
        return pl.ds(pl.multiple_of(start, 8), size)

    started = []

    def push(src, dst, place_to, core_to):
        sem = len(started)
        copy = pltpu.make_async_remote_copy(
            src_ref=src,
            dst_ref=dst,
            send_sem=send.at[sem],
            recv_sem=recv.at[sem],
            device_id=device(place_to, core_to),
            device_id_type=MESH,
        )
        copy.start()
        started.append(copy)
        return copy

    def part_of(q, axis, step):
        return (place[(q + axis) % 3] + step) % 4

    base = [q * CLASS_ROWS + core * size0 for q in classes]
    other = [q * CLASS_ROWS + (1 - core) * size0 for q in classes]
    steps = (2, 1, 3)
    swaps, first, second, third = {}, {}, {}, {}
    for step in steps + (0,):
        for q in classes:
            at = part_of(q, 0, step) * size1
            swaps[q, step] = push(
                part.at[rows(other[q] + at, size1)], half_in.at[q, rows(at, size1)], place, 1 - core
            )
    mine = {}
    for step in steps + (0,):
        for q in classes:
            swaps[q, step].wait_recv()
            at = part_of(q, 0, step) * size1
            value = part[rows(base[q] + at, size1), :] + half_in[q, rows(at, size1), :]
            if step == 0:
                mine[q] = value
                continue
            half[q, rows(at, size1), :] = value
            first[q, step] = push(
                half.at[q, rows(at, size1)],
                q_in.at[q, step - 1],
                moved(place, q % 3, step),
                core,
            )
    for q in classes:
        for step in (1, 3, 2):
            first[q, step].wait_recv()
        quarter[q] = (mine[q] + q_in[q, 0]) + (q_in[q, 1] + q_in[q, 2])
        base[q] = base[q] + part_of(q, 0, 0) * size1
        for step in steps:
            second[q, step] = push(
                quarter.at[q, rows(part_of(q, 1, step) * size2, size2)],
                e_in.at[q, step - 1],
                moved(place, (q + 1) % 3, step),
                core,
            )
    for q in classes:
        for step in (1, 3, 2):
            second[q, step].wait_recv()
        here = part_of(q, 2, 0)
        own = quarter[q, rows(part_of(q, 1, 0) * size2, size2), :]
        p_in[q, here] = (own + e_in[q, 0]) + (e_in[q, 1] + e_in[q, 2])
        for step in steps:
            third[q, step] = push(
                p_in.at[q, here], p_in.at[q, here], moved(place, (q + 2) % 3, step), core
            )
    for q in classes:
        for step in (1, 3, 2):
            third[q, step].wait_recv()
        at = rows(base[q] + part_of(q, 1, 0) * size2, size2)
        total[at, :] = (p_in[q, 0] + p_in[q, 1]) + (p_in[q, 2] + p_in[q, 3])
        for step in steps:
            second[q, step] = push(
                total.at[at], total.at[at], moved(place, (q + 1) % 3, step), core
            )
    last = []
    for q in classes:
        for step in (1, 3, 2):
            second[q, step].wait_recv()
        at = rows(base[q], size1)
        for step in steps:
            first[q, step] = push(total.at[at], total.at[at], moved(place, q % 3, step), core)
        last.append(push(total.at[at], total.at[at], place, 1 - core))
    for step in (1, 3, 2):
        for q in classes:
            first[q, step].wait_recv()
            at = rows(q * CLASS_ROWS + core * size0 + part_of(q, 0, -step) * size1, size1)
            last.append(push(total.at[at], total.at[at], place, 1 - core))
    for copy in last:
        copy.wait_recv()
    for copy in started:
        copy.wait_send()


SENSORS = 600
WIDE = 640
CHUNKS = WIDE // LANES
BLOCKS = [(i, j) for i in range(CHUNKS) for j in range(i, CHUNKS)]
TOP = 16
BLOCK = 48
DIRECTIONS = ((0, 1), (0, -1), (1, 0), (-1, 0), (1, 1), (1, -1), (-1, 1), (-1, -1))


def smooth_kernel(
    adjoint, depth, sensor_row, sensor_column, noise, smoothed_out, operator,
    gram, smoothed, level0, coefficient, levels, total, natural, west, east, low_rows, high_rows,
    low_send, high_send, edge_send, depths, send, recv, load_sem, out_sem, *sums
):
    gx, gy = lax.axis_index("gx"), lax.axis_index("gy")
    sensors, columns, rows = adjoint.shape
    f32, bf16 = jnp.float32, jnp.bfloat16
    loads = []
    for chunk in range(CHUNKS):
        count = min(LANES, sensors - chunk * LANES)
        loads.append(
            pltpu.make_async_copy(
                adjoint.at[pl.ds(chunk * LANES, count)],
                natural.at[chunk, pl.ds(0, count)],
                load_sem.at[chunk],
            )
        )
        loads[-1].start()
    spare = CHUNKS * LANES - sensors
    natural[CHUNKS - 1, pl.ds(LANES - spare, spare)] = jnp.zeros((spare, columns, rows), bf16)

    def neighbour(step):
        return (lax.rem(gx + step[0] + 8, 8), lax.rem(gy + step[1] + 16, 16))

    barrier = pltpu.get_barrier_semaphore()
    for step in DIRECTIONS:
        pl.semaphore_signal(barrier, inc=1, device_id=neighbour(step), device_id_type=MESH)
    greet(barrier, *position())

    upper = lax.broadcasted_iota(jnp.int32, (8, LANES), 0) < 4

    def turn(chunk, half):
        part = natural[chunk, :, pl.ds(pl.multiple_of(half * 16, 16), 16), :]
        level0[pl.ds(half * 16 + 4, 16), chunk, pl.ds(TOP, rows), :] = jnp.transpose(
            part.astype(f32), (1, 2, 0)
        )

    def pack(chunk, group):
        first, last = [], []
        for pair in (0, 1):
            at = group * 4 + pair * 2 + 4
            a, b = [level0[at + odd, chunk, pl.ds(TOP, 8), :] for odd in (0, 1)]
            first.append(jnp.where(upper, a, pltpu.roll(b, 4, 0)))
            a, b = [level0[at + odd, chunk, pl.ds(TOP + rows - 8, 8), :] for odd in (0, 1)]
            last.append(jnp.where(upper, pltpu.roll(a, 4, 0), b))
        at = pl.ds(pl.multiple_of(group * 16, 16), 16)
        low_send[chunk, at, :] = jnp.concatenate(first).astype(bf16)
        high_send[chunk, at, :] = jnp.concatenate(last).astype(bf16)

    def push(src, dst, sem, step):
        copy = pltpu.make_async_remote_copy(
            src_ref=src,
            dst_ref=dst,
            send_sem=send.at[sem],
            recv_sem=recv.at[sem],
            device_id=neighbour(step),
            device_id_type=MESH,
        )
        copy.start()
        return copy

    n4 = columns * 4
    row_copies = []
    depth_copies = []
    for chunk in range(CHUNKS):
        loads[chunk].wait()
        lax.fori_loop(0, columns // 16, lambda half, _: (turn(chunk, half), 0)[1], 0)
        lax.fori_loop(0, columns // 4, lambda group, _: (pack(chunk, group), 0)[1], 0)
        if chunk == 0:
            pl.semaphore_wait(barrier, 18)
            depth_copies = [push(depth, depths.at[k], k, DIRECTIONS[k]) for k in range(8)]
        inner = pl.ds(16, n4)
        row_copies += [
            push(high_send.at[chunk], low_rows.at[chunk, inner], 14 + chunk, (1, 0)),
            push(low_send.at[chunk], high_rows.at[chunk, inner], 19 + chunk, (-1, 0)),
        ]

    def edges(column, _):
        edge_send[column] = level0[column + 4, :, pl.ds(TOP, rows), :].astype(bf16)
        edge_send[column + 4] = level0[column + columns, :, pl.ds(TOP, rows), :].astype(bf16)
        return 0

    lax.fori_loop(0, 4, edges, 0)
    front, back = pl.ds(0, 16), pl.ds(n4 + 16, 16)
    final = pl.ds(n4 - 16, 16)
    halo_copies = [
        push(edge_send.at[pl.ds(4, 4)], west, 8, (0, 1)),
        push(edge_send.at[pl.ds(0, 4)], east, 9, (0, -1)),
        push(high_send.at[:, final], low_rows.at[:, front], 10, (1, 1)),
        push(high_send.at[:, front], low_rows.at[:, back], 11, (1, -1)),
        push(low_send.at[:, final], high_rows.at[:, front], 12, (-1, 1)),
        push(low_send.at[:, front], high_rows.at[:, back], 13, (-1, -1)),
    ]

    site_column = sensor_column[...].reshape(1, sensors) - gy * columns
    site_row = sensor_row[...].reshape(1, sensors) - gx * rows
    sigma = noise[...].reshape(1, sensors)
    pick = lax.broadcasted_iota(jnp.int32, (columns, sensors), 0) == site_column
    along = lax.dot_general(
        depth[...],
        pick.astype(f32),
        (((0,), (0,)), ((), ())),
        precision=lax.Precision.HIGHEST,
        preferred_element_type=f32,
    )
    pick = lax.broadcasted_iota(jnp.int32, (rows, sensors), 0) == site_row
    variance = sigma * sigma * jnp.sum(jnp.where(pick, along, 0.0), axis=0, keepdims=True)
    variance = jnp.concatenate([variance, jnp.zeros((1, spare), f32)], axis=1)

    for copy in depth_copies:
        copy.wait_recv()
    inside_x = {1: gx > 0, -1: gx < 7, 0: gx >= 0}
    inside_y = {1: gy > 0, -1: gy < 15, 0: gy >= 0}

    def tile(step):
        if step == (0, 0):
            return depth[...]
        keep = jnp.logical_and(inside_x[step[0]], inside_y[step[1]])
        return depths[DIRECTIONS.index(step)] * jnp.where(keep, 1.0, 0.0)

    turned = []
    for dx in (1, 0, -1):
        stack = jnp.concatenate(
            [
                tile((dx, 1))[columns - 8 :],
                tile((dx, 0)),
                tile((dx, -1))[:8],
                jnp.zeros((LANES - columns - 16, rows), f32),
            ]
        )
        turned.append(jnp.transpose(stack))
    here = jnp.concatenate([turned[0][rows - TOP :], turned[1], turned[2][:TOP]])
    height = rows + 2 * TOP
    others = (
        pltpu.roll(here, height - 1, 0),
        pltpu.roll(here, 1, 0),
        pltpu.roll(here, LANES - 1, 1),
        pltpu.roll(here, 1, 1),
    )
    weights = [diffusion_step * (0.5 * (here + other)) for other in others]
    kept = [jnp.where(other > 0.0, w, 0.0) for other, w in zip(others, weights)]
    centre = 1.0 - (weights[0] + weights[1] + weights[2] + weights[3])
    for index, value in enumerate([centre] + kept):
        value = value[8 : height - 8]
        for column in range(columns + 6):
            coefficient[index, column] = jnp.broadcast_to(
                value[:, column + 5 : column + 6], (height - 16, LANES)
            )

    def edge(column, _):
        level0[column, :, pl.ds(TOP, rows), :] = west[column].astype(f32)
        level0[column + columns + 4, :, pl.ds(TOP, rows), :] = east[column].astype(f32)
        return 0

    def rims(group, _):
        at = pl.ds(pl.multiple_of(group * 16, 16), 16)
        for chunk in range(CHUNKS):
            low, high = low_rows[chunk, at, :].astype(f32), high_rows[chunk, at, :].astype(f32)
            for pair in (0, 1):
                a, b = low[pair * 8 : pair * 8 + 8], high[pair * 8 : pair * 8 + 8]
                column = group * 4 + pair * 2
                before, after = pl.ds(TOP - 8, 8), pl.ds(TOP + rows, 8)
                level0[column, chunk, before, :] = pltpu.roll(a, 4, 0)
                level0[column + 1, chunk, before, :] = a
                level0[column, chunk, after, :] = b
                level0[column + 1, chunk, after, :] = pltpu.roll(b, 4, 0)
        return 0

    for copy in row_copies:
        copy.wait_recv()
    lax.fori_loop(1, columns // 4 + 1, rims, 0)

    def sweep(read, write, column, first, last):
        for start in range(first, last, BLOCK):
            size = min(BLOCK, last - start)
            k = [coefficient[index, column, pl.ds(8 + start, size), :] for index in range(5)]
            for chunk in range(CHUNKS):
                at = TOP + start
                write(
                    chunk,
                    start,
                    size,
                    k[0] * read(1, chunk, at, size)
                    + k[1] * read(1, chunk, at + 1, size)
                    + k[2] * read(1, chunk, at - 1, size)
                    + k[3] * read(2, chunk, at, size)
                    + k[4] * read(0, chunk, at, size),
                )

    up = columns + 2

    def wave(t, _):
        @pl.when(t == up - 4)
        def _():
            for copy in halo_copies:
                copy.wait_recv()
            lax.fori_loop(0, 4, edge, 0)
            rims(0, 0)
            rims(columns // 4 + 1, 0)

        down = (t >= up).astype(jnp.int32)
        sign = 1 - 2 * down
        first = jnp.where(t >= up, up - t, t + 1)
        order = jnp.where(t >= up, t - up + 2, t + 1)
        near, middle, far = [lax.rem(order + k, 3) for k in (0, 2, 1)]
        slots = (jnp.where(t >= up, near, far), middle, jnp.where(t >= up, far, near))

        def read_first(which, chunk, at, size):
            return level0[first + 3 + which, chunk, pl.ds(at, size), :]

        def read_level(level):
            return lambda which, chunk, at, size: levels[
                down, level, slots[which], chunk, pl.ds(at, size), :
            ]

        def write_level(level):
            def write(chunk, start, size, value):
                levels[down, level, near, chunk, pl.ds(TOP + start, size), :] = value

            return write

        sweep(read_first, write_level(0), first + 3, -8, rows + 8)

        @pl.when(t >= 2)
        def _():
            sweep(read_level(0), write_level(1), first + 3 - sign, -8, rows + 8)

        @pl.when(t >= 4)
        def _():
            sweep(read_level(1), write_level(2), first + 3 - 2 * sign, -8, rows + 8)

        @pl.when(t < 6)
        def _():
            level = lax.div(t, 2)
            levels[1, level, lax.rem(t + 1, 2)] = levels[0, level, near]

        @pl.when(t >= 6)
        def _():
            def write(chunk, start, size, value):
                smoothed[
                    first - 3 * sign, pl.ds(start, size), pl.ds(chunk * LANES, LANES)
                ] = value.astype(bf16)

            sweep(read_level(2), write, first + 3 - 3 * sign, 0, rows)

        return 0

    lax.fori_loop(0, up + 4, wave, 0)
    out_copy = pltpu.make_async_copy(smoothed, smoothed_out, out_sem)
    out_copy.start()

    total[...] = jnp.zeros_like(total)

    def accumulate(group, _):
        part = smoothed[pl.ds(group * 8, 8)].reshape(8 * rows, WIDE)
        for chunk in range(CHUNKS):
            at = chunk * LANES
            total[pl.ds(at, LANES), pl.ds(at, WIDE - at)] += lax.dot_general(
                part[:, at : at + LANES],
                part[:, at:],
                (((0,), (0,)), ((), ())),
                preferred_element_type=f32,
            )
        return 0

    lax.fori_loop(0, columns // 8, accumulate, 0)
    inverse_cells = 1.0 / (columns * rows * 128)
    diagonal = lax.broadcasted_iota(jnp.int32, (LANES, LANES), 0) == lax.broadcasted_iota(
        jnp.int32, (LANES, LANES), 1
    )
    for at, (i, j) in enumerate(BLOCKS):
        value = total[pl.ds(i * LANES, LANES), pl.ds(j * LANES, LANES)] * inverse_cells
        if i == j:
            part = slice(i * LANES, (i + 1) * LANES)
            value = value + jnp.where(diagonal, variance[:, part], 0.0)
        gram[pl.ds(at * LANES, LANES), :] = value
    unused = gram.shape[0] - len(BLOCKS) * LANES
    gram[pl.ds(len(BLOCKS) * LANES, unused), :] = jnp.zeros((unused, LANES), f32)
    all_reduce(gram, operator, *sums)
    out_copy.wait()
    for copy in depth_copies + row_copies + halo_copies:
        copy.wait_send()


def smoothed_and_operator(adjoint, depth, sensor_row, sensor_column, noise):
    vmem = pl.BlockSpec(memory_space=pltpu.VMEM)
    whole = pl.BlockSpec(memory_space=pl.ANY)
    f32, bf16 = jnp.float32, jnp.bfloat16
    _, columns, rows = adjoint.shape
    height = rows + 2 * TOP
    rim = pltpu.VMEM((CHUNKS, (columns + 8) * 4, LANES), bf16)
    return pl.pallas_call(
        smooth_kernel,
        out_shape=(
            jax.ShapeDtypeStruct((columns, rows, WIDE), bf16),
            jax.ShapeDtypeStruct((CLASSES * CLASS_ROWS, LANES), f32),
        ),
        in_specs=[whole] + [vmem] * 4,
        out_specs=(whole, vmem),
        scratch_shapes=[
            pltpu.VMEM((CLASSES * CLASS_ROWS, LANES), f32),
            pltpu.VMEM((columns, rows, WIDE), bf16),
            pltpu.VMEM((columns + 8, CHUNKS, height, LANES), f32),
            pltpu.VMEM((5, columns + 6, height - 16, LANES), f32),
            pltpu.VMEM((2, 3, 3, CHUNKS, height, LANES), f32),
            pltpu.VMEM((WIDE, WIDE), f32),
            pltpu.VMEM((CHUNKS, LANES, columns, rows), bf16),
            pltpu.VMEM((4, CHUNKS, rows, LANES), bf16),
            pltpu.VMEM((4, CHUNKS, rows, LANES), bf16),
            rim,
            rim,
            pltpu.VMEM((CHUNKS, columns * 4, LANES), bf16),
            pltpu.VMEM((CHUNKS, columns * 4, LANES), bf16),
            pltpu.VMEM((8, CHUNKS, rows, LANES), bf16),
            pltpu.VMEM((8, columns, rows), f32),
            pltpu.SemaphoreType.DMA((24,)),
            pltpu.SemaphoreType.DMA((24,)),
            pltpu.SemaphoreType.DMA((CHUNKS,)),
            pltpu.SemaphoreType.DMA,
            pltpu.VMEM((CLASSES, CLASS_ROWS // 2, LANES), f32),
            pltpu.VMEM((CLASSES, 3, CLASS_ROWS // 8, LANES), f32),
            pltpu.VMEM((CLASSES, 3, CLASS_ROWS // 32, LANES), f32),
            pltpu.VMEM((CLASSES, 4, CLASS_ROWS // 32, LANES), f32),
            pltpu.VMEM((CLASSES, CLASS_ROWS // 2, LANES), f32),
            pltpu.VMEM((CLASSES, CLASS_ROWS // 8, LANES), f32),
            pltpu.SemaphoreType.DMA((69,)),
            pltpu.SemaphoreType.DMA((69,)),
        ],
        compiler_params=pltpu.CompilerParams(
            collective_id=1, has_side_effects=True, vmem_limit_bytes=66_000_000
        ),
        name="smooth_and_reduce",
    )(adjoint, depth, sensor_row, sensor_column, noise)


GROUP = 16
PIECES = 4


def split(value):
    high = value.astype(jnp.bfloat16)
    return high, (value - high.astype(jnp.float32)).astype(jnp.bfloat16)


def gain_kernel(stacked, smoothed_in, out, left, right, plane, smoothed, spread, ready, sems):
    f32, bf16 = jnp.float32, jnp.bfloat16
    columns, rows, _ = smoothed.shape
    load = pltpu.make_async_copy(smoothed_in, smoothed, sems.at[0])
    load.start()
    whole = plane.at[1]
    for at, (i, j) in enumerate(BLOCKS):
        block = stacked[pl.ds(at * LANES, LANES), :]
        size = min(LANES, SENSORS - i * LANES)
        whole[pl.ds(i * LANES, size), pl.ds(j * LANES, LANES)] = block[:size]
        if i != j:
            size = min(LANES, SENSORS - j * LANES)
            whole[pl.ds(j * LANES, size), pl.ds(i * LANES, LANES)] = jnp.transpose(block)[:size]
    blocks = [whole[:, chunk * LANES : (chunk + 1) * LANES] for chunk in range(CHUNKS)]
    reach = sum(jnp.sum(jnp.abs(block), axis=1, keepdims=True) for block in blocks)
    scale = 1.0 / jnp.max(reach)
    row = lax.broadcasted_iota(jnp.int32, (SENSORS, LANES), 0)
    lane = lax.broadcasted_iota(jnp.int32, (SENSORS, LANES), 1)
    zeros = jnp.zeros((WIDE - SENSORS, WIDE), bf16)

    def store(at, high, low):
        right[pl.ds(0, SENSORS), at] = high
        right[pl.ds(WIDE, SENSORS), at] = high
        right[pl.ds(2 * WIDE, SENSORS), at] = low

    for k in range(3):
        for half in range(2):
            right[pl.ds(k * WIDE + SENSORS, WIDE - SENSORS), pl.ds(half * WIDE, WIDE)] = zeros
    inverse = plane.at[1]
    for chunk, block in enumerate(blocks):
        diagonal = jnp.where(row == lane + chunk * LANES, 1.0, 0.0)
        residual = diagonal - block * scale
        at = pl.ds(chunk * LANES, LANES)
        plane[0, :, at] = residual
        inverse[:, at] = (diagonal + residual) * scale

    def product(width):
        value = plane[0]
        high, low = split(value)
        left[:, pl.ds(0, WIDE)] = high
        left[:, pl.ds(WIDE, WIDE)] = low
        left[:, pl.ds(2 * WIDE, WIDE)] = high
        store(pl.ds(0, WIDE), high, low)
        if width > WIDE:
            high, low = split(inverse[...])
            store(pl.ds(WIDE, WIDE), high, low)
        return jnp.dot(left[...], right[:, pl.ds(0, width)], preferred_element_type=f32)

    plane[0] = product(WIDE)
    for _ in range(2):
        both = product(2 * WIDE)
        plane[0] = both[:, :WIDE]
        inverse[...] = inverse[...] + both[:, WIDE:]
    high, low = split(plane[0])
    left[:, pl.ds(0, WIDE)] = high
    left[:, pl.ds(WIDE, WIDE)] = low
    left[:, pl.ds(2 * WIDE, WIDE)] = high
    high, low = split(inverse[...])
    store(pl.ds(0, WIDE), high, low)
    final = inverse[...] + jnp.dot(
        left[...], right[:, pl.ds(0, WIDE)], preferred_element_type=f32
    )
    left[:, pl.ds(0, WIDE)] = final.astype(bf16)

    load.wait()
    stores = []
    for group in range(columns // GROUP):
        for pair in range(GROUP // 2):
            field = smoothed[pl.ds(group * GROUP + pair * 2, 2)].reshape(2 * rows, WIDE)
            value = lax.dot_general(
                left[:, pl.ds(0, WIDE)],
                field,
                (((1,), (1,)), ((), ())),
                preferred_element_type=f32,
            )
            for odd in (0, 1):
                spread[pl.ds(pair * 2 + odd, SENSORS, stride=GROUP), :] = value[
                    :, odd * rows : (odd + 1) * rows
                ]
        for piece in range(PIECES):
            size = SENSORS // PIECES
            some = pl.ds(piece * size, size)
            ready[group, some] = (
                spread[pl.ds(piece * size * GROUP, size * GROUP), :]
                .reshape(size, GROUP, rows)
                .astype(bf16)
            )
            stores.append(
                pltpu.make_async_copy(
                    ready.at[group, some],
                    out.at[some, pl.ds(group * GROUP, GROUP), :],
                    sems.at[1 + len(stores)],
                )
            )
            stores[-1].start()
    for store in stores:
        store.wait()


def gains(stacked, smoothed):
    vmem = pl.BlockSpec(memory_space=pltpu.VMEM)
    columns, rows, _ = smoothed.shape
    return pl.pallas_call(
        gain_kernel,
        out_shape=jax.ShapeDtypeStruct((SENSORS, columns, rows), jnp.bfloat16),
        in_specs=[vmem, pl.BlockSpec(memory_space=pl.ANY)],
        out_specs=pl.BlockSpec(memory_space=pl.ANY),
        scratch_shapes=[
            pltpu.VMEM((SENSORS, 3 * WIDE), jnp.bfloat16),
            pltpu.VMEM((3 * WIDE, 2 * WIDE), jnp.bfloat16),
            pltpu.VMEM((2, SENSORS, WIDE), jnp.float32),
            pltpu.VMEM(smoothed.shape, jnp.bfloat16),
            pltpu.VMEM((SENSORS * GROUP, LANES), jnp.float32),
            pltpu.VMEM((columns // GROUP, SENSORS, GROUP, rows), jnp.bfloat16),
            pltpu.SemaphoreType.DMA((1 + columns // GROUP * PIECES,)),
        ],
        compiler_params=pltpu.CompilerParams(vmem_limit_bytes=66_000_000),
        name="inverse_and_gain",
    )(stacked, smoothed)


def local(adjoint, seafloor_depth, sensor_row, sensor_column, noise_sigma):
    smoothed, stacked = smoothed_and_operator(
        adjoint, seafloor_depth, sensor_row, sensor_column, noise_sigma
    )
    return gains(stacked, smoothed)


def solution(mesh):
    in_specs = (P(None, "gy", "gx"), P("gy", "gx"), P(), P(), P())
    out_specs = P(None, "gy", "gx")
    return jax.shard_map(local, mesh=mesh, in_specs=in_specs, out_specs=out_specs, check_vma=False)
```
